32 devices in a mesh: gx: 8 (over z, y), gz: 4 (over x, core).
Axes of the slice: x: 2, y: 2, z: 4, core: 2. Of those that a mesh axis runs over, the one named last changes fastest.
Arguments:
- velocity_field: float32 [3, 3072, 16, 512], P(None, 'gx', None, 'gz'), may hold values from -6 to 6
- interp_weight: bfloat16 [2048, 128, 512], P(('gx', 'gz')), may hold values from -0.25 to 0.25
- particle_velocity: float32 [3, 2048, 128], P(None, ('gx', 'gz')), may hold values from -6 to 6
- tile_owner: int32 [8192, 1], P(('gx', 'gz')), may hold values from 0 to 31; in each aligned block of 256 rows (0 to 255, 256 to 511, ...) at most 24 rows name the same one
- tile_index: int32 [8192], P(('gx', 'gz')), may hold values from 0 to 6143
- block_count: int32 [32], P(('gx', 'gz')), may hold values from 16 to 64, as said below
Outputs:
- fluid_rhs: float32 [3, 3072, 16, 512], P(None, 'gx', None, 'gz')
- new_velocity: float32 [3, 2048, 128], P(None, ('gx', 'gz'))
The draws below stay inside these ranges and needn't reach their ends.
Inputs may be any that keep to these rules, and one draw needn't show every extreme that they name: `tile_owner`: among the 256 requests of one device, no owner is named more than 24 times, a bound that some block reaches. `block_count`: some device has all 64 blocks live.
All inputs are finite; a program needn't handle non-finite values.
Results may differ from the reference program's by a relative error of at most 0.0014.
Values may be sent and summed in bfloat16 or wider, within the bound.
A program may use at most 256 MiB of HBM per device.

```python
import math
import jax
import jax.numpy as jnp
import numpy as np
from jax import lax

CX = 384
CY = 16
CZ = 128
PB = 128
BLK_DEV = 64
KT = 4
REQ_DEV = 256
CAP = 24
NX = 3072
NY = 16
NZ = 512
BLOCKS = 2048
REQS = 8192
N_GX = 8
N_GZ = 4
DEVICES = 32


def draw_block_count(key, part):
    devices = N_GX * N_GZ
    fewest = max(1, BLK_DEV // 4)
    counts = jax.random.randint(jax.random.fold_in(key, 11), (devices,), fewest, BLK_DEV + 1)
    full_at = jax.random.randint(jax.random.fold_in(key, 12), (), 0, devices)
    other_at = (full_at + 1 + jax.random.randint(jax.random.fold_in(key, 13), (), 0, devices - 1)) % devices
    counts = counts.at[full_at].set(BLK_DEV).at[other_at].set(fewest)
    return counts.astype(jnp.int32)


def touch_ends(result, rng, low, top_value):
    index_at = [jax.random.randint(jax.random.fold_in(rng, axis), (), 0, length) for axis, length in enumerate(result.shape)]
    widest = result.shape.index(max(result.shape))
    beside = index_at[:widest] + [(index_at[widest] + 1) % result.shape[widest]] + index_at[widest + 1:]
    return result.at[tuple(index_at)].set(low).at[tuple(beside)].set(top_value)


def block_levels(own_key, shape, split, low, largest):
    def one(axis_at, parts):
        heights = jax.random.uniform(jax.random.fold_in(jax.random.fold_in(own_key, 6), axis_at), (parts,), jnp.float32, low / len(split), largest / len(split))
        return jnp.repeat(jnp.exp(heights), shape[axis_at] // parts).reshape((-1,) + (1,) * (len(shape) - axis_at - 1))

    loudness = one(*split[0])
    for cut in split[1:]:
        loudness = loudness * one(*cut)
    return loudness


def deal_out(rng, own, number, rows, count, top, limit, slope):
    sequence = jax.random.permutation(rng, count)
    crowded, usual = portions_of(count, rows * top, limit, slope, True), portions_of(count, rows * top, limit, slope, False)
    places = jnp.arange(count)

    def named(lengths, turn):
        used = int((lengths > 0).sum())
        fixed = max(1, used // 4)
        passed = fixed + (places - fixed + turn * (used - fixed)) % max(1, count - fixed)
        return jnp.zeros((count,), jnp.int32).at[sequence[jnp.where(places < fixed, places, passed)]].set(jnp.asarray(lengths, jnp.int32))

    lengths = jnp.where(number % 4 == 0, named(crowded, number // 4), named(usual, number - number // 4 - 1))
    mixed = jax.random.permutation(jax.random.fold_in(own, 3), count)
    giver, receiver = mixed[0:count // 2 * 2:2], mixed[1:count // 2 * 2:2]
    slack = jnp.minimum(lengths[giver] - 1, limit - lengths[receiver]) // 2
    slack = jnp.where((giver == sequence[0]) | (receiver == sequence[0]) | (lengths[receiver] == 0), 0, jnp.maximum(slack, 0))
    passed = jax.random.randint(jax.random.fold_in(own, 4), (count // 2,), 0, 1 << 20) % (slack + 1)
    lengths = lengths.at[giver].add(-passed).at[receiver].add(passed)
    labels = jnp.searchsorted(jnp.cumsum(lengths), jnp.arange(rows * top), side="right").astype(jnp.int32)
    table = labels.reshape(top, rows).T
    table = table[jax.random.permutation(jax.random.fold_in(own, 1), rows)]
    turn = jax.random.randint(jax.random.fold_in(own, 2), (rows, 1), 0, top)
    return jnp.take_along_axis(table, (jnp.arange(top)[None, :] + turn) % top, axis=1)


def portions_of(number_of, total, limit, skew, full):
    weights = [(1 << 20) // math.isqrt(standing ** skew) + 1 for standing in range(1, number_of + 1)]
    largest = limit if full else min(limit, max(-(-total // number_of), total * weights[0] // sum(weights)))
    least = 1 if total - largest >= number_of - 1 else 0
    given, surplus = [largest] + [least] * (number_of - 1), total - largest - least * (number_of - 1)
    while surplus > 0:
        free = [i for i in range(1, number_of) if given[i] < largest] or [i for i in range(1, number_of) if given[i] < limit]
        pool, left = sum([weights[i] for i in free]), surplus
        for i in free:
            addition = min(limit - given[i], max(1, left * weights[i] // pool), surplus)
            given[i] = given[i] + addition
            surplus = surplus - addition
    return np.array(given)


def bell_draw(rng, dims, spread, bound, cuts=(), kind=jnp.bfloat16):
    array = spread * jax.random.normal(rng, dims, jnp.float32)
    if cuts:
        array = array * block_levels(rng, dims, cuts, -0.22, 0.18)
    return jnp.clip(array, -bound, bound).astype(kind)


def setup_inputs(seed: int = 0) -> dict:
    streams_of = jax.random.split(jax.random.key(seed), 7)
    velocity_field = bell_draw(streams_of[0], (3, NX, NY, NZ), 1.0, 6.0, ((1, 8), (3, 4)), jnp.float32)
    interp_weight = bell_draw(streams_of[1], (BLOCKS, PB, KT * CZ), (KT * CZ) ** -0.5, 0.25, ((0, 32),))
    particle_velocity = bell_draw(streams_of[2], (3, BLOCKS, PB), 1.0, 6.0, ((1, 32),), jnp.float32)
    tile_owner_keys = jax.random.split(jax.random.fold_in(streams_of[3], 1), REQS // REQ_DEV)
    tile_owner_turns = jax.random.permutation(jax.random.fold_in(streams_of[3], 3), REQS // REQ_DEV)
    tile_owner = jax.vmap(lambda own, number: deal_out(jax.random.fold_in(streams_of[3], 2), own, number, REQ_DEV, DEVICES, 1, CAP, 2))(tile_owner_keys, tile_owner_turns).reshape((REQS, 1))
    tile_index = touch_ends(jax.random.randint(streams_of[4], (REQS,), 0, CX * CY), jax.random.fold_in(streams_of[4], 1), 0, (CX * CY) - 1).astype(jnp.int32)
    block_count = draw_block_count(jax.random.fold_in(streams_of[6], 71), 0)
    return dict(velocity_field=velocity_field, interp_weight=interp_weight, particle_velocity=particle_velocity, tile_owner=tile_owner, tile_index=tile_index, block_count=block_count)


ALPHA = 1.0 / 3.0
A_COEF = 14.0 / 9.0
B_COEF = 1.0 / 9.0
VISCOSITY = 0.2
RELAX_TIME = 1.0
TIME_STEP = 0.5
LOADING = 0.5


def derivative(field):
    length = field.shape[0]
    wavenum = jnp.arange(length // 2 + 1).astype(field.dtype) * (2.0 * math.pi / length)
    symbol = (A_COEF * jnp.sin(wavenum) + 0.5 * B_COEF * jnp.sin(2.0 * wavenum)) / (1.0 + 2.0 * ALPHA * jnp.cos(wavenum))
    spectrum = jnp.fft.rfft(field, axis=0)
    return jnp.fft.irfft(spectrum * (1j * symbol)[:, None, None], n=length, axis=0).astype(field.dtype)


def particle_step(items):
    weights, tile_data, velocity, live_mask = items
    wide = weights.astype(jnp.float32)
    sampled = jnp.einsum("bpm,cbm->cbp", wide, tile_data.astype(jnp.float32), precision=lax.Precision.HIGHEST)
    drag_accel = live_mask[None, :, None] * (sampled - velocity) / RELAX_TIME
    new_velocity = velocity + TIME_STEP * drag_accel
    drag_half = lax.optimization_barrier(drag_accel.astype(jnp.bfloat16))
    push_back = -LOADING * jnp.einsum("bpm,cbp->cbm", wide, drag_half.astype(jnp.float32), precision=lax.Precision.HIGHEST)
    return new_velocity, push_back


def reference(velocity_field, interp_weight, particle_velocity, tile_owner, tile_index, block_count):
    devices = N_GX * N_GZ
    stream_comp = velocity_field[0]
    pieces = []
    for axis_comp in range(3):
        component = velocity_field[axis_comp]
        advect = 0.5 * (derivative(stream_comp * component) + stream_comp * derivative(component))
        span_curve = jnp.roll(component, -1, 2) - 2.0 * component + jnp.roll(component, 1, 2)
        pieces.append(-advect + VISCOSITY * span_curve)
    fluid = jnp.stack(pieces)
    owners = tile_owner[:, 0]
    slab_row = (owners // N_GZ) * CX + tile_index // CY
    wall_row = tile_index % CY
    span_piece = owners % N_GZ
    blocked = velocity_field.reshape(3, NX, NY, N_GZ, CZ)
    tile_data = blocked[:, slab_row, wall_row, span_piece, :].astype(jnp.bfloat16)
    tile_data = tile_data.reshape(3, devices, BLK_DEV, KT * CZ).transpose(1, 0, 2, 3)
    weights = interp_weight.reshape(devices, BLK_DEV, PB, KT * CZ)
    velocity = particle_velocity.reshape(3, devices, BLK_DEV, PB).transpose(1, 0, 2, 3)
    live_mask = (jnp.arange(BLK_DEV, dtype=jnp.int32)[None, :] < block_count[:, None]).astype(velocity_field.dtype)
    moved, push_back = lax.map(particle_step, (weights, tile_data, velocity, live_mask))
    new_velocity = moved.transpose(1, 0, 2, 3).reshape(3, devices * BLK_DEV, PB)
    push_back = push_back.transpose(1, 0, 2, 3).reshape(3, devices * BLK_DEV * KT, CZ)
    feedback = jnp.zeros((3, NX, NY, N_GZ, CZ), velocity_field.dtype).at[:, slab_row, wall_row, span_piece, :].add(push_back)
    fluid_rhs = fluid + feedback.reshape(3, NX, NY, NZ)
    return fluid_rhs, new_velocity
```

```python
import functools
import math

import jax
import jax.numpy as jnp
from jax import lax
from jax.experimental import pallas as pl
from jax.experimental.pallas import tpu as pltpu
from jax.sharding import PartitionSpec as P

ROOT = (math.sqrt(5.0) / 3.0 - 1.0) * 1.5
GREEN_GAIN = 3.0 / math.sqrt(5.0)
GAMMA = (25.0 / 36.0) * GREEN_GAIN * (1.0 - ROOT * ROOT)
EPS = (1.0 / 12.0) / GAMMA
VISCOSITY = 0.2
RELAX_TIME = 1.0
TIME_STEP = 0.5
LOADING = 0.5
WINDOW = 96
F32 = jnp.float32
BF16 = jnp.bfloat16
VMEM_LIMIT = 56 * 1024 * 1024


def iota(shape, dim):
    return lax.broadcasted_iota(jnp.int32, shape, dim)


def dot(a, b, ca, cb):
    return lax.dot_general(a, b, (((ca,), (cb,)), ((), ())), preferred_element_type=F32)


def prep_kernel(kt, capacity, owner_ref, index_ref, send_ref, slot_ref):
    count = owner_ref.shape[1]
    devices = send_ref.shape[0]
    blocks = count // kt
    rows, cols = iota((count, count), 0), iota((count, count), 1)
    pick = cols == kt * (rows % blocks) + rows // blocks
    owner = jnp.sum(jnp.where(pick, owner_ref[...], 0), 1, keepdims=True)
    index = jnp.sum(jnp.where(pick, index_ref[...], 0), 1, keepdims=True)
    named = owner == iota((count, devices), 1)
    onehot = named.astype(F32)
    lower = (cols <= rows).astype(F32).astype(BF16)
    seen = dot(lower, onehot.astype(BF16), 1, 0)
    position = jnp.sum(seen * onehot, 1, keepdims=True).astype(jnp.int32) - 1
    slot_ref[...] = owner * capacity + position
    place = position == iota((count, capacity), 1)
    high = jnp.where(place, (index // 128).astype(F32), 0.0).astype(BF16)
    low = jnp.where(place, (index % 128).astype(F32), 0.0).astype(BF16)
    turned = onehot.astype(BF16)
    high_sum, low_sum = dot(turned, high, 0, 0), dot(turned, low, 0, 0)
    send_ref[...] = high_sum.astype(jnp.int32) * 128 + low_sum.astype(jnp.int32)


def row_fields(ref, i):
    u = [ref[c, i] for c in range(3)]
    return u + [u[0] * u[c] for c in range(3)]


def edge_kernel(u_ref, right_ref, left_ref, low_ref, high_ref):
    step, last = pl.program_id(0), pl.num_programs(0) - 1
    window, wall, span = u_ref.shape[1:]
    shape = (8, span)
    pick = jnp.where(
        ((iota(shape, 0) == 0) & (iota(shape, 1) == 0))
        | ((iota(shape, 0) == 1) & (iota(shape, 1) == span - 1)),
        1.0,
        0.0,
    ).astype(BF16)
    for c in range(3):
        cells = u_ref[c].reshape(window * wall, span).astype(BF16)
        lanes = dot(pick, cells, 1, 1)
        low_ref[c] = lanes[0:1].astype(BF16)
        high_ref[c] = lanes[1:2].astype(BF16)

    def body(order):
        def one(i, state):
            fields = row_fields(u_ref, order(i))
            return tuple(f + ROOT * s for f, s in zip(fields, state))

        return lax.fori_loop(0, window, one, (jnp.zeros((wall, span), F32),) * 6, unroll=4)

    @pl.when(step == last)
    def _():
        for k, value in enumerate(body(lambda i: i)):
            right_ref[k] = value
        for c in range(3):
            right_ref[6 + c] = u_ref[c, window - 1]

    @pl.when(step == 0)
    def _():
        for k, value in enumerate(body(lambda i: window - 1 - i)):
            left_ref[k] = value
        for c in range(3):
            left_ref[6 + c] = u_ref[c, 0]


def gather_kernel(index_ref, field_ref, out_ref, rows_ref):
    count = out_ref.shape[0]
    span = field_ref.shape[2]

    def one(r, carry):
        row = index_ref[0, r]
        for c in range(3):
            rows_ref[c, pl.ds(r, 1), :] = field_ref[c, pl.ds(row, 1), :]
        return carry

    lax.fori_loop(0, count, one, 0, unroll=8)
    for c in range(3):
        out_ref[:, c * span : (c + 1) * span] = rows_ref[c].astype(BF16)


def deriv_kernel(u_ref, low_ref, high_ref, left_ref, right_ref, out_ref, state_ref, part_ref, halo_ref):
    step = pl.program_id(0)
    blocks = pl.num_programs(0) // 2
    rows, wall, span = u_ref.shape[1:]
    lane = iota((wall, span), 1)

    def load_state(edge_ref):
        edge = [edge_ref[6 + c] for c in range(3)]
        edge = edge + [edge[0] * edge[c] for c in range(3)]
        for k in range(6):
            state_ref[k] = edge_ref[k]
            state_ref[6 + k] = edge[k]

    @pl.when(step == 0)
    def _():
        load_state(left_ref)

    @pl.when(step == blocks)
    def _():
        load_state(right_ref)

    def advance(i, carry):
        state, before = carry[:6], carry[6:]
        fields = row_fields(u_ref, i)
        parts = [EPS * f + s for f, s in zip(before, state)]
        sums = [parts[3 + c] + fields[0] * parts[c] for c in range(3)]
        moved = [f + ROOT * s for f, s in zip(fields, state)]
        return fields, sums, tuple(moved) + tuple(fields)

    start = tuple(state_ref[k] for k in range(12))

    @pl.when(step < blocks)
    def _():
        shape = (8, rows * wall)
        corner = (8, span)
        pick = jnp.where(
            ((iota(corner, 0) == 0) & (iota(corner, 1) == 0))
            | ((iota(corner, 0) == 1) & (iota(corner, 1) == span - 1)),
            VISCOSITY,
            0.0,
        )
        for c in range(3):
            ends = jnp.where(
                iota(shape, 0) == 0,
                low_ref[c].astype(F32),
                jnp.where(iota(shape, 0) == 1, high_ref[c].astype(F32), 0.0),
            )
            halo_ref[c] = dot(ends, pick.astype(F32) / VISCOSITY, 0, 0).reshape(rows, wall, span)

        def one(i, carry):
            fields, sums, carry = advance(i, carry)
            for c in range(3):
                u = fields[c]
                near = jnp.where(lane == 0, 0.0, pltpu.roll(u, 1, 1))
                far = jnp.where(lane == span - 1, 0.0, pltpu.roll(u, span - 1, 1))
                curve = near + far + halo_ref[c, i] - 2.0 * u
                part_ref[c, step * rows + i] = 0.5 * GAMMA * sums[c] + VISCOSITY * curve
            return carry

        end = lax.fori_loop(0, rows, one, start, unroll=4)
        for k in range(12):
            state_ref[k] = end[k]

    @pl.when(step >= blocks)
    def _():
        block = 2 * blocks - 1 - step

        def one(n, carry):
            i = rows - 1 - n
            _, sums, carry = advance(i, carry)
            for c in range(3):
                out_ref[c, i] = part_ref[c, block * rows + i] - 0.5 * GAMMA * sums[c]
            return carry

        end = lax.fori_loop(0, rows, one, start, unroll=4)
        for k in range(12):
            state_ref[k] = end[k]


def particle_kernel(kt, live_ref, slot_ref, reply_ref, weight_ref, velocity_ref, moved_ref, out_ref, own_ref, push_ref):
    step, last = pl.program_id(0), pl.num_programs(0) - 1
    group, particles, cells = weight_ref.shape
    count, slots = slot_ref.shape[0], reply_ref.shape[0]
    span = cells // kt
    blocks = count // kt

    @pl.when(step == 0)
    def _():
        chosen = jnp.where(slot_ref[...] == iota((count, slots), 1), 1.0, 0.0).astype(BF16)
        own = dot(chosen, reply_ref[...], 1, 0)
        for j in range(kt):
            for c in range(3):
                own_ref[c, :, j * span : (j + 1) * span] = own[
                    j * blocks : (j + 1) * blocks, c * span : (c + 1) * span
                ]

    base = pl.multiple_of(step * group, group)
    tiles = jnp.concatenate([own_ref[c, pl.ds(base, group), :] for c in range(3)], 0).astype(BF16)
    row = iota((3 * group, particles), 0) % group
    sampled = jnp.zeros((3 * group, particles), F32)
    for b in range(group):
        sampled = jnp.where(row == b, dot(tiles, weight_ref[b], 1, 1), sampled)
    velocity = velocity_ref[...].reshape(3 * group, particles)
    live = jnp.where(row + base < live_ref[0], 1.0, 0.0)
    drag = live * (sampled - velocity) * (1.0 / RELAX_TIME)
    moved_ref[...] = (velocity + TIME_STEP * drag).reshape(3, group, particles)
    half = drag.astype(BF16)
    row = iota((3 * group, cells), 0) % group
    push = jnp.zeros((3 * group, cells), F32)
    for b in range(group):
        push = jnp.where(row == b, dot(half, weight_ref[b], 1, 0), push)
    push = -LOADING * push
    for j in range(kt):
        for c in range(3):
            push_ref[pl.ds(j * blocks + base, group), c * span : (c + 1) * span] = push[
                c * group : (c + 1) * group, j * span : (j + 1) * span
            ]

    @pl.when(step == last)
    def _():
        same = iota((count, count), 0) == iota((count, count), 1)
        slot_row = jnp.sum(jnp.where(same, slot_ref[...], 0), 0, keepdims=True)
        placed = jnp.where(iota((slots, count), 0) == slot_row, 1.0, 0.0).astype(BF16)
        out_ref[...] = dot(placed, push_ref[...].astype(BF16), 1, 0).astype(BF16)


def add_kernel(index_ref, base_ref, back_ref, out_ref):
    rows, span = base_ref.shape[1:]
    slots = back_ref.shape[0]
    ids = iota((rows, slots), 0) + pl.program_id(0) * rows
    named = jnp.where(ids == index_ref[...], 1.0, 0.0).astype(BF16)
    total = dot(named, back_ref[...], 1, 0)
    for c in range(3):
        out_ref[c] = base_ref[c] + total[:, c * span : (c + 1) * span]


def vmem():
    return pl.BlockSpec(memory_space=pltpu.VMEM)


def smem():
    return pl.BlockSpec(memory_space=pltpu.SMEM)


def params():
    return pltpu.CompilerParams(vmem_limit_bytes=VMEM_LIMIT)


def cost(flops, nbytes):
    return pl.CostEstimate(flops=int(flops), bytes_accessed=int(nbytes), transcendentals=0)


def largest_divisor(total, limit):
    return max(d for d in range(1, limit + 1) if total % d == 0)


def shards(velocity_field, interp_weight, particle_velocity, tile_owner, tile_index, block_count):
    _, slab, wall, span = velocity_field.shape
    shape = jax.ShapeDtypeStruct
    gx, gz = lax.axis_size("gx"), lax.axis_size("gz")
    devices = gx * gz
    requests = tile_index.shape[0]
    blocks, particles, cells = interp_weight.shape
    kt = requests // blocks
    capacity = max(2, 3 * requests // devices)
    slots = devices * capacity
    field_bytes = velocity_field.size * 4

    send_index, slot_ids = pl.pallas_call(
        functools.partial(prep_kernel, kt, capacity),
        out_shape=(shape((devices, capacity), jnp.int32), shape((requests, 1), jnp.int32)),
        in_specs=[vmem(), vmem()],
        out_specs=(vmem(), vmem()),
        cost_estimate=cost(1e7, 1e5),
        name="prep",
    )(tile_owner.reshape(1, requests), tile_index.reshape(1, requests))
    got = lax.all_to_all(send_index, ("gx", "gz"), split_axis=0, concat_axis=0, tiled=True)
    got = got.reshape(1, slots)

    window = WINDOW if slab % WINDOW == 0 else slab
    lines = slab * wall
    to_right, to_left, low, high = pl.pallas_call(
        edge_kernel,
        grid=(slab // window,),
        out_shape=(shape((9, wall, span), F32),) * 2 + (shape((3, 1, lines), BF16),) * 2,
        in_specs=[pl.BlockSpec((3, window, wall, span), lambda i: (0, i, 0, 0))],
        out_specs=(pl.BlockSpec((9, wall, span), lambda i: (0, 0, 0)),) * 2
        + (pl.BlockSpec((3, 1, window * wall), lambda i: (0, 0, i)),) * 2,
        compiler_params=params(),
        cost_estimate=cost(1e7, field_bytes),
        name="edges",
    )(velocity_field)
    ahead = lambda n: [(i, (i + 1) % n) for i in range(n)]
    behind = lambda n: [((i + 1) % n, i) for i in range(n)]
    from_left = lax.ppermute(to_right, "gx", ahead(gx))
    from_right = lax.ppermute(to_left, "gx", behind(gx))
    from_low = lax.ppermute(high, "gz", ahead(gz))
    from_high = lax.ppermute(low, "gz", behind(gz))

    tile_data = pl.pallas_call(
        gather_kernel,
        out_shape=shape((slots, 3 * span), BF16),
        in_specs=[smem(), vmem()],
        out_specs=vmem(),
        scratch_shapes=[pltpu.VMEM((3, slots, span), F32)],
        compiler_params=params(),
        cost_estimate=cost(1e6, field_bytes),
        name="gather",
    )(got, velocity_field.reshape(3, lines, span))
    replies = lax.all_to_all(tile_data, ("gx", "gz"), split_axis=0, concat_axis=0, tiled=True)

    rows = largest_divisor(slab, 48)
    parts = slab // rows
    fluid = pl.pallas_call(
        deriv_kernel,
        grid=(2 * parts,),
        out_shape=shape(velocity_field.shape, F32),
        in_specs=[
            pl.BlockSpec((3, rows, wall, span), lambda i: (0, jnp.minimum(i, 2 * parts - 1 - i), 0, 0)),
            pl.BlockSpec((3, 1, rows * wall), lambda i: (0, 0, jnp.minimum(i, parts - 1))),
            pl.BlockSpec((3, 1, rows * wall), lambda i: (0, 0, jnp.minimum(i, parts - 1))),
            pl.BlockSpec((9, wall, span), lambda i: (0, 0, 0)),
            pl.BlockSpec((9, wall, span), lambda i: (0, 0, 0)),
        ],
        out_specs=pl.BlockSpec(
            (3, rows, wall, span), lambda i: (0, jnp.minimum(parts - 1, 2 * parts - 1 - i), 0, 0)
        ),
        scratch_shapes=[
            pltpu.VMEM((12, wall, span), F32),
            pltpu.VMEM((3, slab, wall, span), F32),
            pltpu.VMEM((3, rows, wall, span), F32),
        ],
        compiler_params=params(),
        cost_estimate=cost(velocity_field.size * 40, field_bytes * 3),
        name="deriv",
    )(velocity_field, from_low, from_high, from_left, from_right)

    group = 8
    moved, outgoing = pl.pallas_call(
        functools.partial(particle_kernel, kt),
        grid=(blocks // group,),
        out_shape=(shape(particle_velocity.shape, F32), shape((slots, 3 * span), BF16)),
        in_specs=[
            smem(),
            pl.BlockSpec((requests, 1), lambda i: (0, 0)),
            pl.BlockSpec((slots, 3 * span), lambda i: (0, 0)),
            pl.BlockSpec((group, particles, cells), lambda i: (i, 0, 0)),
            pl.BlockSpec((3, group, particles), lambda i: (0, i, 0)),
        ],
        out_specs=(
            pl.BlockSpec((3, group, particles), lambda i: (0, i, 0)),
            pl.BlockSpec((slots, 3 * span), lambda i: (0, 0)),
        ),
        scratch_shapes=[
            pltpu.VMEM((3, blocks, cells), F32),
            pltpu.VMEM((requests, 3 * span), F32),
        ],
        compiler_params=params(),
        cost_estimate=cost(4e8, interp_weight.size * 2),
        name="particles",
    )(block_count, slot_ids, replies, interp_weight, particle_velocity)
    returned = lax.all_to_all(outgoing, ("gx", "gz"), split_axis=0, concat_axis=0, tiled=True)

    chunk = largest_divisor(lines, 512)
    result = pl.pallas_call(
        add_kernel,
        grid=(lines // chunk,),
        out_shape=shape((3, lines, span), F32),
        in_specs=[
            pl.BlockSpec((1, slots), lambda i: (0, 0)),
            pl.BlockSpec((3, chunk, span), lambda i: (0, i, 0)),
            pl.BlockSpec((slots, 3 * span), lambda i: (0, 0)),
        ],
        out_specs=pl.BlockSpec((3, chunk, span), lambda i: (0, i, 0)),
        compiler_params=params(),
        cost_estimate=cost(2.0 * lines * slots * 3 * span, field_bytes * 2),
        name="feedback",
    )(got, fluid.reshape(3, lines, span), returned)
    return (result.reshape(velocity_field.shape), moved)


def solution(mesh):
    placed = (
        P(None, "gx", None, "gz"),
        P(("gx", "gz"), None, None),
        P(None, ("gx", "gz"), None),
        P(("gx", "gz"), None),
        P(("gx", "gz")),
        P(("gx", "gz")),
    )
    return jax.shard_map(
        shards,
        mesh=mesh,
        in_specs=placed,
        out_specs=(P(None, "gx", None, "gz"), P(None, ("gx", "gz"), None)),
        check_vma=False,
    )
```

```python
import functools
import math

import jax
import jax.numpy as jnp
from jax import lax
from jax.experimental import pallas as pl
from jax.experimental.pallas import tpu as pltpu
from jax.sharding import PartitionSpec as P

ROOT = (math.sqrt(5.0) / 3.0 - 1.0) * 1.5
GREEN_GAIN = 3.0 / math.sqrt(5.0)
GAMMA = (25.0 / 36.0) * GREEN_GAIN * (1.0 - ROOT * ROOT)
EPS = (1.0 / 12.0) / GAMMA
VISCOSITY = 0.2
RELAX_TIME = 1.0
TIME_STEP = 0.5
LOADING = 0.5
WINDOW = 96
F32 = jnp.float32
BF16 = jnp.bfloat16
VMEM_LIMIT = 56 * 1024 * 1024


def iota(shape, dim):
    return lax.broadcasted_iota(jnp.int32, shape, dim)


def dot(a, b, ca, cb):
    return lax.dot_general(a, b, (((ca,), (cb,)), ((), ())), preferred_element_type=F32)


def end_lanes(span):
    corner = (8, span)
    first = (iota(corner, 0) == 0) & (iota(corner, 1) == 0)
    second = (iota(corner, 0) == 1) & (iota(corner, 1) == span - 1)
    return jnp.where(first | second, 1.0, 0.0)


def request_slots(kt, capacity, devices, owner_row, index_row):
    count = owner_row.shape[1]
    blocks = count // kt
    rows, cols = iota((count, count), 0), iota((count, count), 1)
    pick = cols == kt * (rows % blocks) + rows // blocks
    owner = jnp.sum(jnp.where(pick, owner_row, 0), 1, keepdims=True)
    index = jnp.sum(jnp.where(pick, index_row, 0), 1, keepdims=True)
    onehot = (owner == iota((count, devices), 1)).astype(F32)
    lower = (cols <= rows).astype(F32).astype(BF16)
    seen = dot(lower, onehot.astype(BF16), 1, 0)
    position = jnp.sum(seen * onehot, 1, keepdims=True).astype(jnp.int32) - 1
    place = position == iota((count, 128), 1)
    high = jnp.where(place, (index // 128).astype(F32), 0.0).astype(BF16)
    low = jnp.where(place, (index % 128).astype(F32), 0.0).astype(BF16)
    turned = onehot.astype(BF16)
    high_sum, low_sum = dot(turned, high, 0, 0), dot(turned, low, 0, 0)
    send = high_sum.astype(jnp.int32) * 128 + low_sum.astype(jnp.int32)
    return owner * capacity + position, send


def row_fields(ref, i):
    u = [ref[c, i] for c in range(3)]
    return u + [u[0] * u[c] for c in range(3)]


def exchange_kernel(
    sizes, owner_ref, index_ref, field_hbm,
    tile_ref, slot_ref, got_ref, low_ref, high_ref, left_ref, right_ref,
    field_ref, table_ref, send_ref, got_smem, rows_ref, my_low, my_high, my_left, my_right,
    field_sem, smem_sem, send_sem, recv_sem, edge_send, edge_recv,
):
    gx, gz, kt, capacity, window = sizes
    devices = gx * gz
    wall, span = my_left.shape[1:]
    lines = field_ref.shape[1]
    slab = lines // wall
    x, z = lax.axis_index("gx"), lax.axis_index("gz")
    me = x * gz + z
    fetch = pltpu.make_async_copy(field_hbm, field_ref, field_sem)
    fetch.start()

    barrier = pltpu.get_barrier_semaphore()

    def greet(d, carry):
        peer = lax.rem(me + d, devices)
        pl.semaphore_signal(
            barrier, inc=1, device_id=(peer // gz, lax.rem(peer, gz)), device_id_type=pl.DeviceIdType.MESH
        )
        return carry

    lax.fori_loop(1, devices, greet, 0)
    slot, send = request_slots(kt, capacity, devices, owner_ref[...], index_ref[...])
    slot_ref[...] = slot
    table_ref[...] = send
    for d in range(devices):
        send_ref[d] = table_ref[d : d + 1, :]
    pl.semaphore_wait(barrier, devices - 1)

    def parcel(d):
        peer = lax.rem(me + d, devices)
        return pltpu.make_async_remote_copy(
            src_ref=send_ref.at[peer],
            dst_ref=got_ref.at[me],
            send_sem=send_sem.at[d],
            recv_sem=recv_sem.at[d],
            device_id=(peer // gz, lax.rem(peer, gz)),
            device_id_type=pl.DeviceIdType.MESH,
        )

    def post(d, carry):
        parcel(d).start()
        return carry

    lax.fori_loop(1, devices, post, 0)
    got_ref[me] = send_ref[me]
    fetch.wait()

    def edge(k, src, dst, peer):
        return pltpu.make_async_remote_copy(
            src_ref=src,
            dst_ref=dst,
            send_sem=edge_send.at[k],
            recv_sem=edge_recv.at[k],
            device_id=peer,
            device_id_type=pl.DeviceIdType.MESH,
        )

    edges = [
        edge(0, my_right, left_ref, (lax.rem(x + 1, gx), z)),
        edge(1, my_left, right_ref, (lax.rem(x + gx - 1, gx), z)),
        edge(2, my_high, low_ref, (x, lax.rem(z + 1, gz))),
        edge(3, my_low, high_ref, (x, lax.rem(z + gz - 1, gz))),
    ]

    def moments(order):
        def one(i, state):
            at = pl.ds(pl.multiple_of(order(i) * wall, wall), wall)
            u = [field_ref[c, at, :] for c in range(3)]
            fields = u + [u[0] * u[c] for c in range(3)]
            return tuple(f + ROOT * s for f, s in zip(fields, state))

        return lax.fori_loop(0, window, one, (jnp.zeros((wall, span), F32),) * 6, unroll=4)

    for k, value in enumerate(moments(lambda i: slab - window + i)):
        my_right[k] = value
    for c in range(3):
        my_right[6 + c] = field_ref[c, lines - wall :, :]
    edges[0].start()
    for k, value in enumerate(moments(lambda i: window - 1 - i)):
        my_left[k] = value
    for c in range(3):
        my_left[6 + c] = field_ref[c, :wall, :]
    edges[1].start()

    def arrive(d, carry):
        parcel(d).wait()
        return carry

    lax.fori_loop(1, devices, arrive, 0)
    copy = pltpu.make_async_copy(got_ref, got_smem, smem_sem)
    copy.start()
    copy.wait()

    def gather(d, carry):
        for k in range(capacity):
            row = jnp.minimum(jnp.maximum(got_smem[d, 0, k], 0), lines - 1)
            for c in range(3):
                rows_ref[c, pl.ds(d * capacity + k, 1), :] = field_ref[c, pl.ds(row, 1), :]
        return carry

    lax.fori_loop(0, devices, gather, 0)
    for c in range(3):
        tile_ref[:, c * span : (c + 1) * span] = rows_ref[c].astype(BF16)

    pick = end_lanes(span).astype(BF16)
    for c in range(3):
        for n in range(slab // window):
            part = slice(n * window * wall, (n + 1) * window * wall)
            lanes = dot(pick, field_ref[c, part].astype(BF16), 1, 1)
            my_low[c, :, part] = lanes[0:1]
            my_high[c, :, part] = lanes[1:2]
    edges[2].start()
    edges[3].start()
    for copy in edges:
        copy.wait()


def load_state(state_ref, edge_ref):
    edge = [edge_ref[6 + c] for c in range(3)]
    edge = edge + [edge[0] * edge[c] for c in range(3)]
    for k in range(6):
        state_ref[k] = edge_ref[k]
        state_ref[6 + k] = edge[k]


def advance(u_ref, i, carry):
    state, before = carry[:6], carry[6:]
    fields = row_fields(u_ref, i)
    parts = [EPS * f + s for f, s in zip(before, state)]
    sums = [parts[3 + c] + fields[0] * parts[c] for c in range(3)]
    moved = [f + ROOT * s for f, s in zip(fields, state)]
    return fields, sums, tuple(moved) + tuple(fields)


def up_kernel(u_ref, low_ref, high_ref, left_ref, out_ref, state_ref, halo_ref):
    rows, wall, span = u_ref.shape[1:]
    lane = iota((wall, span), 1)

    @pl.when(pl.program_id(0) == 0)
    def _():
        load_state(state_ref, left_ref)

    shape = (8, rows * wall)
    pick = end_lanes(span)
    for c in range(3):
        ends = jnp.where(iota(shape, 0) == 0, low_ref[c], jnp.where(iota(shape, 0) == 1, high_ref[c], 0.0))
        halo_ref[c] = dot(ends, pick, 0, 0).reshape(rows, wall, span)

    def one(i, carry):
        fields, sums, carry = advance(u_ref, i, carry)
        for c in range(3):
            u = fields[c]
            near = jnp.where(lane == 0, 0.0, pltpu.roll(u, 1, 1))
            far = jnp.where(lane == span - 1, 0.0, pltpu.roll(u, span - 1, 1))
            curve = near + far + halo_ref[c, i] - 2.0 * u
            out_ref[c, i] = 0.5 * GAMMA * sums[c] + VISCOSITY * curve
        return carry

    end = lax.fori_loop(0, rows, one, tuple(state_ref[k] for k in range(12)), unroll=4)
    for k in range(12):
        state_ref[k] = end[k]


def down_kernel(u_ref, part_ref, right_ref, out_ref, state_ref):
    rows = u_ref.shape[1]

    @pl.when(pl.program_id(0) == 0)
    def _():
        load_state(state_ref, right_ref)

    def one(n, carry):
        i = rows - 1 - n
        _, sums, carry = advance(u_ref, i, carry)
        for c in range(3):
            out_ref[c, i] = part_ref[c, i] - 0.5 * GAMMA * sums[c]
        return carry

    end = lax.fori_loop(0, rows, one, tuple(state_ref[k] for k in range(12)), unroll=4)
    for k in range(12):
        state_ref[k] = end[k]


def particle_kernel(kt, live_ref, slot_ref, reply_ref, weight_ref, velocity_ref, moved_ref, out_ref, own_ref, push_ref):
    step, last = pl.program_id(0), pl.num_programs(0) - 1
    group, particles, cells = weight_ref.shape
    count, slots = slot_ref.shape[0], reply_ref.shape[0]
    span = cells // kt
    blocks = count // kt

    @pl.when(step == 0)
    def _():
        chosen = jnp.where(slot_ref[...] == iota((count, slots), 1), 1.0, 0.0).astype(BF16)
        own = dot(chosen, reply_ref[...], 1, 0)
        for j in range(kt):
            for c in range(3):
                own_ref[c, :, j * span : (j + 1) * span] = own[
                    j * blocks : (j + 1) * blocks, c * span : (c + 1) * span
                ]

    base = pl.multiple_of(step * group, group)
    tiles = jnp.concatenate([own_ref[c, pl.ds(base, group), :] for c in range(3)], 0).astype(BF16)
    row = iota((3 * group, particles), 0) % group
    sampled = jnp.zeros((3 * group, particles), F32)
    for b in range(group):
        sampled = jnp.where(row == b, dot(tiles, weight_ref[b], 1, 1), sampled)
    velocity = velocity_ref[...].reshape(3 * group, particles)
    live = jnp.where(row + base < live_ref[0], 1.0, 0.0)
    drag = live * (sampled - velocity) * (1.0 / RELAX_TIME)
    moved_ref[...] = (velocity + TIME_STEP * drag).reshape(3, group, particles)
    half = drag.astype(BF16)
    row = iota((3 * group, cells), 0) % group
    push = jnp.zeros((3 * group, cells), F32)
    for b in range(group):
        push = jnp.where(row == b, dot(half, weight_ref[b], 1, 0), push)
    push = -LOADING * push
    for j in range(kt):
        for c in range(3):
            push_ref[pl.ds(j * blocks + base, group), c * span : (c + 1) * span] = push[
                c * group : (c + 1) * group, j * span : (j + 1) * span
            ]

    @pl.when(step == last)
    def _():
        same = iota((count, count), 0) == iota((count, count), 1)
        slot_row = jnp.sum(jnp.where(same, slot_ref[...], 0), 0, keepdims=True)
        placed = jnp.where(iota((slots, count), 0) == slot_row, 1.0, 0.0).astype(BF16)
        out_ref[...] = dot(placed, push_ref[...].astype(BF16), 1, 0).astype(BF16)


def add_kernel(index_ref, base_ref, back_ref, out_ref):
    rows, span = base_ref.shape[1:]
    slots = back_ref.shape[0]
    for n in range(rows // 256):
        local = index_ref[...] - (pl.program_id(0) * rows + n * 256)
        local = jnp.where((local >= 0) & (local < 256), local, -1).astype(F32).astype(BF16)
        ids = iota((256, slots), 0).astype(F32).astype(BF16)
        named = jnp.where(ids == local, jnp.ones((), BF16), jnp.zeros((), BF16))
        total = dot(named, back_ref[...], 1, 0)
        part = slice(n * 256, (n + 1) * 256)
        for c in range(3):
            out_ref[c, part] = base_ref[c, part] + total[:, c * span : (c + 1) * span]


def vmem():
    return pl.BlockSpec(memory_space=pltpu.VMEM)


def smem():
    return pl.BlockSpec(memory_space=pltpu.SMEM)


def params():
    return pltpu.CompilerParams(vmem_limit_bytes=VMEM_LIMIT)


def cost(flops, nbytes):
    return pl.CostEstimate(flops=int(flops), bytes_accessed=int(nbytes), transcendentals=0)


def largest_divisor(total, limit):
    return max(d for d in range(1, limit + 1) if total % d == 0)


def shards(velocity_field, interp_weight, particle_velocity, tile_owner, tile_index, block_count):
    _, slab, wall, span = velocity_field.shape
    shape = jax.ShapeDtypeStruct
    gx, gz = lax.axis_size("gx"), lax.axis_size("gz")
    devices = gx * gz
    requests = tile_index.shape[0]
    blocks, particles, cells = interp_weight.shape
    kt = requests // blocks
    capacity = max(2, 3 * requests // devices)
    slots = devices * capacity
    field_bytes = velocity_field.size * 4

    window = WINDOW if slab % WINDOW == 0 else slab
    lines = slab * wall
    dma = pltpu.SemaphoreType.DMA
    tile_data, slot_ids, got, from_low, from_high, from_left, from_right = pl.pallas_call(
        functools.partial(exchange_kernel, (gx, gz, kt, capacity, window)),
        out_shape=(
            shape((slots, 3 * span), BF16),
            shape((requests, 1), jnp.int32),
            shape((devices, 1, 128), jnp.int32),
            shape((3, 1, lines), F32),
            shape((3, 1, lines), F32),
            shape((9, wall, span), F32),
            shape((9, wall, span), F32),
        ),
        in_specs=[vmem(), vmem(), pl.BlockSpec(memory_space=pl.ANY)],
        out_specs=(vmem(),) * 7,
        scratch_shapes=[
            pltpu.VMEM((3, lines, span), F32),
            pltpu.VMEM((devices, 128), jnp.int32),
            pltpu.VMEM((devices, 1, 128), jnp.int32),
            pltpu.SMEM((devices, 1, 128), jnp.int32),
            pltpu.VMEM((3, slots, span), F32),
            pltpu.VMEM((3, 1, lines), F32),
            pltpu.VMEM((3, 1, lines), F32),
            pltpu.VMEM((9, wall, span), F32),
            pltpu.VMEM((9, wall, span), F32),
            dma,
            dma,
            dma((devices,)),
            dma((devices,)),
            dma((4,)),
            dma((4,)),
        ],
        compiler_params=pltpu.CompilerParams(
            vmem_limit_bytes=VMEM_LIMIT, collective_id=0, has_side_effects=True
        ),
        cost_estimate=cost(1e7, field_bytes),
        name="exchange",
    )(tile_owner.reshape(1, requests), tile_index.reshape(1, requests), velocity_field.reshape(3, lines, span))
    got = got[:, 0, :capacity].reshape(1, slots)
    replies = lax.all_to_all(tile_data, ("gx", "gz"), split_axis=0, concat_axis=0, tiled=True)

    rows = largest_divisor(slab, 48)
    parts = slab // rows
    up_part = pl.pallas_call(
        up_kernel,
        grid=(parts,),
        out_shape=shape(velocity_field.shape, F32),
        in_specs=[
            pl.BlockSpec((3, rows, wall, span), lambda i: (0, i, 0, 0)),
            pl.BlockSpec((3, 1, rows * wall), lambda i: (0, 0, i)),
            pl.BlockSpec((3, 1, rows * wall), lambda i: (0, 0, i)),
            pl.BlockSpec((9, wall, span), lambda i: (0, 0, 0)),
        ],
        out_specs=pl.BlockSpec((3, rows, wall, span), lambda i: (0, i, 0, 0)),
        scratch_shapes=[pltpu.VMEM((12, wall, span), F32), pltpu.VMEM((3, rows, wall, span), F32)],
        compiler_params=params(),
        cost_estimate=cost(velocity_field.size * 20, field_bytes * 2),
        name="up",
    )(velocity_field, from_low, from_high, from_left)
    replies, up_part = lax.optimization_barrier((replies, up_part))

    group = 8
    moved, outgoing = pl.pallas_call(
        functools.partial(particle_kernel, kt),
        grid=(blocks // group,),
        out_shape=(shape(particle_velocity.shape, F32), shape((slots, 3 * span), BF16)),
        in_specs=[
            smem(),
            pl.BlockSpec((requests, 1), lambda i: (0, 0)),
            pl.BlockSpec((slots, 3 * span), lambda i: (0, 0)),
            pl.BlockSpec((group, particles, cells), lambda i: (i, 0, 0)),
            pl.BlockSpec((3, group, particles), lambda i: (0, i, 0)),
        ],
        out_specs=(
            pl.BlockSpec((3, group, particles), lambda i: (0, i, 0)),
            pl.BlockSpec((slots, 3 * span), lambda i: (0, 0)),
        ),
        scratch_shapes=[
            pltpu.VMEM((3, blocks, cells), F32),
            pltpu.VMEM((requests, 3 * span), F32),
        ],
        compiler_params=params(),
        cost_estimate=cost(4e8, interp_weight.size * 2),
        name="particles",
    )(block_count, slot_ids, replies, interp_weight, particle_velocity)
    outgoing, up_part = lax.optimization_barrier((outgoing, up_part))
    returned = lax.all_to_all(outgoing, ("gx", "gz"), split_axis=0, concat_axis=0, tiled=True)
    fluid = pl.pallas_call(
        down_kernel,
        grid=(parts,),
        out_shape=shape(velocity_field.shape, F32),
        in_specs=[
            pl.BlockSpec((3, rows, wall, span), lambda i: (0, parts - 1 - i, 0, 0)),
            pl.BlockSpec((3, rows, wall, span), lambda i: (0, parts - 1 - i, 0, 0)),
            pl.BlockSpec((9, wall, span), lambda i: (0, 0, 0)),
        ],
        out_specs=pl.BlockSpec((3, rows, wall, span), lambda i: (0, parts - 1 - i, 0, 0)),
        scratch_shapes=[pltpu.VMEM((12, wall, span), F32)],
        compiler_params=params(),
        cost_estimate=cost(velocity_field.size * 20, field_bytes * 3),
        name="down",
    )(velocity_field, up_part, from_right)

    chunk = 512 if lines % 512 == 0 else lines
    result = pl.pallas_call(
        add_kernel,
        grid=(lines // chunk,),
        out_shape=shape((3, lines, span), F32),
        in_specs=[
            pl.BlockSpec((1, slots), lambda i: (0, 0)),
            pl.BlockSpec((3, chunk, span), lambda i: (0, i, 0)),
            pl.BlockSpec((slots, 3 * span), lambda i: (0, 0)),
        ],
        out_specs=pl.BlockSpec((3, chunk, span), lambda i: (0, i, 0)),
        compiler_params=params(),
        cost_estimate=cost(2.0 * lines * slots * 3 * span, field_bytes * 2),
        name="feedback",
    )(got, fluid.reshape(3, lines, span), returned)
    return (result.reshape(velocity_field.shape), moved)


def solution(mesh):
    placed = (
        P(None, "gx", None, "gz"),
        P(("gx", "gz"), None, None),
        P(None, ("gx", "gz"), None),
        P(("gx", "gz"), None),
        P(("gx", "gz")),
        P(("gx", "gz")),
    )
    return jax.shard_map(
        shards,
        mesh=mesh,
        in_specs=placed,
        out_specs=(P(None, "gx", None, "gz"), P(None, ("gx", "gz"), None)),
        check_vma=False,
    )
```

```python
import functools
import math

import jax
import jax.numpy as jnp
from jax import lax
from jax.experimental import pallas as pl
from jax.experimental.pallas import tpu as pltpu
from jax.sharding import PartitionSpec as P

ROOT = (math.sqrt(5.0) / 3.0 - 1.0) * 1.5
GREEN_GAIN = 3.0 / math.sqrt(5.0)
GAMMA = (25.0 / 36.0) * GREEN_GAIN * (1.0 - ROOT * ROOT)
EPS = (1.0 / 12.0) / GAMMA
VISCOSITY = 0.2
RELAX_TIME = 1.0
TIME_STEP = 0.5
LOADING = 0.5
WINDOW = 96
F32 = jnp.float32
BF16 = jnp.bfloat16
VMEM_LIMIT = 56 * 1024 * 1024


def iota(shape, dim):
    return lax.broadcasted_iota(jnp.int32, shape, dim)


def dot(a, b, ca, cb):
    return lax.dot_general(a, b, (((ca,), (cb,)), ((), ())), preferred_element_type=F32)


def end_lanes(span):
    corner = (8, span)
    first = (iota(corner, 0) == 0) & (iota(corner, 1) == 0)
    second = (iota(corner, 0) == 1) & (iota(corner, 1) == span - 1)
    return jnp.where(first | second, 1.0, 0.0)


def request_slots(kt, capacity, devices, owner_row, index_row):
    count = owner_row.shape[1]
    blocks = count // kt
    rows, cols = iota((count, count), 0), iota((count, count), 1)
    pick = cols == kt * (rows % blocks) + rows // blocks
    owner = jnp.sum(jnp.where(pick, owner_row, 0), 1, keepdims=True)
    index = jnp.sum(jnp.where(pick, index_row, 0), 1, keepdims=True)
    onehot = (owner == iota((count, devices), 1)).astype(F32)
    lower = (cols <= rows).astype(F32).astype(BF16)
    seen = dot(lower, onehot.astype(BF16), 1, 0)
    position = jnp.sum(seen * onehot, 1, keepdims=True).astype(jnp.int32) - 1
    place = position == iota((count, 128), 1)
    high = jnp.where(place, (index // 128).astype(F32), 0.0).astype(BF16)
    low = jnp.where(place, (index % 128).astype(F32), 0.0).astype(BF16)
    turned = onehot.astype(BF16)
    high_sum, low_sum = dot(turned, high, 0, 0), dot(turned, low, 0, 0)
    send = high_sum.astype(jnp.int32) * 128 + low_sum.astype(jnp.int32)
    return owner * capacity + position, send


def row_fields(ref, i):
    u = [ref[c, i] for c in range(3)]
    return u + [u[0] * u[c] for c in range(3)]


def exchange_kernel(
    sizes, owner_ref, index_ref, field_hbm,
    reply_ref, slot_ref, got_ref, right_ref, part_hbm,
    field_ref, table_ref, send_ref, got_smem, rows_ref, tile_ref, my_low, my_high, my_left, my_right,
    low_ref, high_ref, left_ref, halo_ref, part_ref,
    field_sem, smem_sem, send_sem, recv_sem, tile_send, tile_recv, edge_send, edge_recv, part_sem,
):
    gx, gz, kt, capacity, window = sizes
    devices = gx * gz
    wall, span = my_left.shape[1:]
    lines = field_ref.shape[1]
    slab = lines // wall
    x, z = lax.axis_index("gx"), lax.axis_index("gz")
    me = x * gz + z
    fetch = pltpu.make_async_copy(field_hbm, field_ref, field_sem)
    fetch.start()

    barrier = pltpu.get_barrier_semaphore()

    def greet(d, carry):
        peer = lax.rem(me + d, devices)
        pl.semaphore_signal(
            barrier, inc=1, device_id=(peer // gz, lax.rem(peer, gz)), device_id_type=pl.DeviceIdType.MESH
        )
        return carry

    lax.fori_loop(1, devices, greet, 0)
    slot, send = request_slots(kt, capacity, devices, owner_ref[...], index_ref[...])
    slot_ref[...] = slot
    table_ref[...] = send
    for d in range(devices):
        send_ref[d] = table_ref[d : d + 1, :]
    pl.semaphore_wait(barrier, devices - 1)

    def parcel(d):
        peer = lax.rem(me + d, devices)
        return pltpu.make_async_remote_copy(
            src_ref=send_ref.at[peer],
            dst_ref=got_ref.at[me],
            send_sem=send_sem.at[d],
            recv_sem=recv_sem.at[d],
            device_id=(peer // gz, lax.rem(peer, gz)),
            device_id_type=pl.DeviceIdType.MESH,
        )

    def post(d, carry):
        parcel(d).start()
        return carry

    lax.fori_loop(1, devices, post, 0)
    got_ref[me] = send_ref[me]
    fetch.wait()

    def arrive(d, carry):
        parcel(d).wait()
        return carry

    lax.fori_loop(1, devices, arrive, 0)
    copy = pltpu.make_async_copy(got_ref, got_smem, smem_sem)
    copy.start()
    copy.wait()

    def collect(peer):
        for k in range(capacity):
            row = jnp.minimum(jnp.maximum(got_smem[peer, 0, k], 0), lines - 1)
            for c in range(3):
                rows_ref[c, k : k + 1, :] = field_ref[c, pl.ds(row, 1), :]
        return [rows_ref[c].astype(BF16) for c in range(3)]

    def tiles(d):
        peer = lax.rem(me + d, devices)
        return pltpu.make_async_remote_copy(
            src_ref=tile_ref.at[peer],
            dst_ref=reply_ref.at[me],
            send_sem=tile_send.at[d],
            recv_sem=tile_recv.at[d],
            device_id=(peer // gz, lax.rem(peer, gz)),
            device_id_type=pl.DeviceIdType.MESH,
        )

    def gather(d, carry):
        peer = lax.rem(me + d, devices)
        for c, value in enumerate(collect(peer)):
            tile_ref[peer, :, c * span : (c + 1) * span] = value
        tiles(d).start()
        return carry

    lax.fori_loop(1, devices, gather, 0)
    for c, value in enumerate(collect(me)):
        reply_ref[me, :, c * span : (c + 1) * span] = value

    def edge(k, src, dst, peer):
        return pltpu.make_async_remote_copy(
            src_ref=src,
            dst_ref=dst,
            send_sem=edge_send.at[k],
            recv_sem=edge_recv.at[k],
            device_id=peer,
            device_id_type=pl.DeviceIdType.MESH,
        )

    edges = [
        edge(0, my_right, left_ref, (lax.rem(x + 1, gx), z)),
        edge(1, my_left, right_ref, (lax.rem(x + gx - 1, gx), z)),
        edge(2, my_high, low_ref, (x, lax.rem(z + 1, gz))),
        edge(3, my_low, high_ref, (x, lax.rem(z + gz - 1, gz))),
    ]

    def load(i):
        at = pl.ds(pl.multiple_of(i * wall, wall), wall)
        u = [field_ref[c, at, :] for c in range(3)]
        return u + [u[0] * u[c] for c in range(3)]

    def moments(order):
        def one(i, state):
            return tuple(f + ROOT * s for f, s in zip(load(order(i)), state))

        return lax.fori_loop(0, window, one, (jnp.zeros((wall, span), F32),) * 6, unroll=4)

    for k, value in enumerate(moments(lambda i: slab - window + i)):
        my_right[k] = value
    for c in range(3):
        my_right[6 + c] = field_ref[c, lines - wall :, :]
    edges[0].start()
    pick = end_lanes(span).astype(BF16)
    for c in range(3):
        for n in range(slab // window):
            part = slice(n * window * wall, (n + 1) * window * wall)
            lanes = dot(pick, field_ref[c, part].astype(BF16), 1, 1)
            my_low[c, :, part] = lanes[0:1]
            my_high[c, :, part] = lanes[1:2]
    edges[2].start()
    edges[3].start()
    for k, value in enumerate(moments(lambda i: window - 1 - i)):
        my_left[k] = value
    for c in range(3):
        my_left[6 + c] = field_ref[c, :wall, :]
    edges[1].start()
    for k in (0, 2, 3):
        edges[k].wait()

    rows = halo_ref.shape[1] // wall
    lane = iota((wall, span), 1)
    shape = (8, rows * wall)
    first, second = iota(shape, 0) == 0, iota(shape, 0) == 1

    def leave(n):
        at = pl.ds(pl.multiple_of(n * rows * wall, rows * wall), rows * wall)
        return pltpu.make_async_copy(part_ref.at[:, at, :], part_hbm.at[:, at, :], part_sem.at[n])

    def chunk(n, carry):
        at = pl.ds(pl.multiple_of(n * rows * wall, rows * wall), rows * wall)
        for c in range(3):
            ends = jnp.where(first, low_ref[c, :, at], jnp.where(second, high_ref[c, :, at], 0.0))
            halo_ref[c] = dot(ends.astype(BF16), pick, 0, 0)

        def one(i, carry):
            fields, sums, carry = advance(load(n * rows + i), carry)
            here = pl.ds(pl.multiple_of((n * rows + i) * wall, wall), wall)
            for c in range(3):
                u = fields[c]
                near = jnp.where(lane == 0, 0.0, pltpu.roll(u, 1, 1))
                far = jnp.where(lane == span - 1, 0.0, pltpu.roll(u, span - 1, 1))
                edge_part = halo_ref[c, pl.ds(pl.multiple_of(i * wall, wall), wall), :]
                curve = near + far + edge_part - 2.0 * u
                part_ref[c, here, :] = 0.5 * GAMMA * sums[c] + VISCOSITY * curve
            return carry

        carry = lax.fori_loop(0, rows, one, carry, unroll=4)
        leave(n).start()
        return carry

    border = [left_ref[6 + c] for c in range(3)]
    border = border + [border[0] * border[c] for c in range(3)]
    lax.fori_loop(0, slab // rows, chunk, tuple(left_ref[k] for k in range(6)) + tuple(border))

    def finish(n, carry):
        leave(n).wait()
        return carry

    lax.fori_loop(0, slab // rows, finish, 0)
    edges[1].wait()

    def receive(d, carry):
        tiles(d).wait()
        return carry

    lax.fori_loop(1, devices, receive, 0)


def load_state(state_ref, edge_ref):
    edge = [edge_ref[6 + c] for c in range(3)]
    edge = edge + [edge[0] * edge[c] for c in range(3)]
    for k in range(6):
        state_ref[k] = edge_ref[k]
        state_ref[6 + k] = edge[k]


def advance(fields, carry):
    state, before = carry[:6], carry[6:]
    parts = [EPS * f + s for f, s in zip(before, state)]
    sums = [parts[3 + c] + fields[0] * parts[c] for c in range(3)]
    moved = [f + ROOT * s for f, s in zip(fields, state)]
    return fields, sums, tuple(moved) + tuple(fields)


def down_kernel(u_ref, part_ref, right_ref, out_ref, state_ref):
    rows = u_ref.shape[1]

    @pl.when(pl.program_id(0) == 0)
    def _():
        load_state(state_ref, right_ref)

    def one(n, carry):
        i = rows - 1 - n
        _, sums, carry = advance(row_fields(u_ref, i), carry)
        for c in range(3):
            out_ref[c, i] = part_ref[c, i] - 0.5 * GAMMA * sums[c]
        return carry

    end = lax.fori_loop(0, rows, one, tuple(state_ref[k] for k in range(12)), unroll=4)
    for k in range(12):
        state_ref[k] = end[k]


def particle_kernel(kt, live_ref, slot_ref, reply_ref, weight_ref, velocity_ref, moved_ref, out_ref, own_ref, push_ref):
    step, last = pl.program_id(0), pl.num_programs(0) - 1
    group, particles, cells = weight_ref.shape
    count, slots = slot_ref.shape[0], reply_ref.shape[0]
    span = cells // kt
    blocks = count // kt

    @pl.when(step == 0)
    def _():
        chosen = jnp.where(slot_ref[...] == iota((count, slots), 1), 1.0, 0.0).astype(BF16)
        own = dot(chosen, reply_ref[...], 1, 0)
        for j in range(kt):
            for c in range(3):
                own_ref[c, :, j * span : (j + 1) * span] = own[
                    j * blocks : (j + 1) * blocks, c * span : (c + 1) * span
                ]

    base = pl.multiple_of(step * group, group)
    tiles = jnp.concatenate([own_ref[c, pl.ds(base, group), :] for c in range(3)], 0).astype(BF16)
    row = iota((3 * group, particles), 0) % group
    sampled = jnp.zeros((3 * group, particles), F32)
    for b in range(0, group, 2):
        both = dot(tiles, weight_ref[b : b + 2].reshape(2 * particles, cells), 1, 1)
        sampled = jnp.where(row == b, both[:, :particles], sampled)
        sampled = jnp.where(row == b + 1, both[:, particles:], sampled)
    velocity = velocity_ref[...].reshape(3 * group, particles)
    live = jnp.where(row + base < live_ref[0], 1.0, 0.0)
    drag = live * (sampled - velocity) * (1.0 / RELAX_TIME)
    moved_ref[...] = (velocity + TIME_STEP * drag).reshape(3, group, particles)
    half = drag.astype(BF16)
    row = iota((3 * group, cells), 0) % group
    push = jnp.zeros((3 * group, cells), F32)
    for b in range(group):
        push = jnp.where(row == b, dot(half, weight_ref[b], 1, 0), push)
    push = -LOADING * push
    for j in range(kt):
        for c in range(3):
            push_ref[pl.ds(j * blocks + base, group), c * span : (c + 1) * span] = push[
                c * group : (c + 1) * group, j * span : (j + 1) * span
            ]

    @pl.when(step == last)
    def _():
        same = iota((count, count), 0) == iota((count, count), 1)
        slot_row = jnp.sum(jnp.where(same, slot_ref[...], 0), 0, keepdims=True)
        placed = jnp.where(iota((slots, count), 0) == slot_row, 1.0, 0.0).astype(BF16)
        out_ref[...] = dot(placed, push_ref[...].astype(BF16), 1, 0).astype(BF16)


def add_kernel(index_ref, base_ref, back_ref, out_ref):
    rows, span = base_ref.shape[1:]
    slots = back_ref.shape[0]
    for n in range(rows // 256):
        local = index_ref[...] - (pl.program_id(0) * rows + n * 256)
        local = jnp.where((local >= 0) & (local < 256), local, -1).astype(F32).astype(BF16)
        ids = iota((256, slots), 0).astype(F32).astype(BF16)
        named = jnp.where(ids == local, jnp.ones((), BF16), jnp.zeros((), BF16))
        total = dot(named, back_ref[...], 1, 0)
        part = slice(n * 256, (n + 1) * 256)
        for c in range(3):
            out_ref[c, part] = base_ref[c, part] + total[:, c * span : (c + 1) * span]


def vmem():
    return pl.BlockSpec(memory_space=pltpu.VMEM)


def smem():
    return pl.BlockSpec(memory_space=pltpu.SMEM)


def params():
    return pltpu.CompilerParams(vmem_limit_bytes=VMEM_LIMIT)


def cost(flops, nbytes):
    return pl.CostEstimate(flops=int(flops), bytes_accessed=int(nbytes), transcendentals=0)


def largest_divisor(total, limit):
    return max(d for d in range(1, limit + 1) if total % d == 0)


def shards(velocity_field, interp_weight, particle_velocity, tile_owner, tile_index, block_count):
    _, slab, wall, span = velocity_field.shape
    shape = jax.ShapeDtypeStruct
    gx, gz = lax.axis_size("gx"), lax.axis_size("gz")
    devices = gx * gz
    requests = tile_index.shape[0]
    blocks, particles, cells = interp_weight.shape
    kt = requests // blocks
    capacity = max(2, 3 * requests // devices)
    slots = devices * capacity
    field_bytes = velocity_field.size * 4

    window = WINDOW if slab % WINDOW == 0 else slab
    lines = slab * wall
    dma = pltpu.SemaphoreType.DMA
    rows = largest_divisor(slab, 48)
    parts = slab // rows
    replies, slot_ids, got, from_right, up_part = pl.pallas_call(
        functools.partial(exchange_kernel, (gx, gz, kt, capacity, window)),
        out_shape=(
            shape((devices, capacity, 3 * span), BF16),
            shape((requests, 1), jnp.int32),
            shape((devices, 1, 128), jnp.int32),
            shape((9, wall, span), F32),
            shape((3, lines, span), F32),
        ),
        in_specs=[vmem(), vmem(), pl.BlockSpec(memory_space=pl.ANY)],
        out_specs=(vmem(),) * 4 + (pl.BlockSpec(memory_space=pl.ANY),),
        scratch_shapes=[
            pltpu.VMEM((3, lines, span), F32),
            pltpu.VMEM((devices, 128), jnp.int32),
            pltpu.VMEM((devices, 1, 128), jnp.int32),
            pltpu.SMEM((devices, 1, 128), jnp.int32),
            pltpu.VMEM((3, capacity, span), F32),
            pltpu.VMEM((devices, capacity, 3 * span), BF16),
            pltpu.VMEM((3, 1, lines), F32),
            pltpu.VMEM((3, 1, lines), F32),
            pltpu.VMEM((9, wall, span), F32),
            pltpu.VMEM((9, wall, span), F32),
            pltpu.VMEM((3, 1, lines), F32),
            pltpu.VMEM((3, 1, lines), F32),
            pltpu.VMEM((9, wall, span), F32),
            pltpu.VMEM((3, rows * wall, span), F32),
            pltpu.VMEM((3, lines, span), F32),
            dma,
            dma,
            dma((devices,)),
            dma((devices,)),
            dma((devices,)),
            dma((devices,)),
            dma((4,)),
            dma((4,)),
            dma((parts,)),
        ],
        compiler_params=pltpu.CompilerParams(
            vmem_limit_bytes=VMEM_LIMIT, collective_id=0, has_side_effects=True
        ),
        cost_estimate=cost(1e7, field_bytes),
        name="exchange",
    )(tile_owner.reshape(1, requests), tile_index.reshape(1, requests), velocity_field.reshape(3, lines, span))
    got = got[:, 0, :capacity].reshape(1, slots)
    replies = replies.reshape(slots, 3 * span)
    up_part = up_part.reshape(velocity_field.shape)

    group = 16 if blocks % 16 == 0 else 8
    moved, outgoing = pl.pallas_call(
        functools.partial(particle_kernel, kt),
        grid=(blocks // group,),
        out_shape=(shape(particle_velocity.shape, F32), shape((slots, 3 * span), BF16)),
        in_specs=[
            smem(),
            pl.BlockSpec((requests, 1), lambda i: (0, 0)),
            pl.BlockSpec((slots, 3 * span), lambda i: (0, 0)),
            pl.BlockSpec((group, particles, cells), lambda i: (i, 0, 0)),
            pl.BlockSpec((3, group, particles), lambda i: (0, i, 0)),
        ],
        out_specs=(
            pl.BlockSpec((3, group, particles), lambda i: (0, i, 0)),
            pl.BlockSpec((slots, 3 * span), lambda i: (0, 0)),
        ),
        scratch_shapes=[
            pltpu.VMEM((3, blocks, cells), F32),
            pltpu.VMEM((requests, 3 * span), F32),
        ],
        compiler_params=params(),
        cost_estimate=cost(4e8, interp_weight.size * 2),
        name="particles",
    )(block_count, slot_ids, replies, interp_weight, particle_velocity)
    outgoing, up_part = lax.optimization_barrier((outgoing, up_part))
    returned = lax.all_to_all(outgoing, ("gx", "gz"), split_axis=0, concat_axis=0, tiled=True)
    fluid = pl.pallas_call(
        down_kernel,
        grid=(parts,),
        out_shape=shape(velocity_field.shape, F32),
        in_specs=[
            pl.BlockSpec((3, rows, wall, span), lambda i: (0, parts - 1 - i, 0, 0)),
            pl.BlockSpec((3, rows, wall, span), lambda i: (0, parts - 1 - i, 0, 0)),
            pl.BlockSpec((9, wall, span), lambda i: (0, 0, 0)),
        ],
        out_specs=pl.BlockSpec((3, rows, wall, span), lambda i: (0, parts - 1 - i, 0, 0)),
        scratch_shapes=[pltpu.VMEM((12, wall, span), F32)],
        compiler_params=params(),
        cost_estimate=cost(velocity_field.size * 20, field_bytes * 3),
        name="down",
    )(velocity_field, up_part, from_right)

    chunk = 2048 if lines % 2048 == 0 else lines
    result = pl.pallas_call(
        add_kernel,
        grid=(lines // chunk,),
        out_shape=shape((3, lines, span), F32),
        in_specs=[
            pl.BlockSpec((1, slots), lambda i: (0, 0)),
            pl.BlockSpec((3, chunk, span), lambda i: (0, i, 0)),
            pl.BlockSpec((slots, 3 * span), lambda i: (0, 0)),
        ],
        out_specs=pl.BlockSpec((3, chunk, span), lambda i: (0, i, 0)),
        compiler_params=params(),
        cost_estimate=cost(2.0 * lines * slots * 3 * span, field_bytes * 2),
        name="feedback",
    )(got, fluid.reshape(3, lines, span), returned)
    return (result.reshape(velocity_field.shape), moved)


def solution(mesh):
    placed = (
        P(None, "gx", None, "gz"),
        P(("gx", "gz"), None, None),
        P(None, ("gx", "gz"), None),
        P(("gx", "gz"), None),
        P(("gx", "gz")),
        P(("gx", "gz")),
    )
    return jax.shard_map(
        shards,
        mesh=mesh,
        in_specs=placed,
        out_specs=(P(None, "gx", None, "gz"), P(None, ("gx", "gz"), None)),
        check_vma=False,
    )
```

```python
import functools
import math

import jax
import jax.numpy as jnp
from jax import lax
from jax.experimental import pallas as pl
from jax.experimental.pallas import tpu as pltpu
from jax.sharding import PartitionSpec as P

ROOT = (math.sqrt(5.0) / 3.0 - 1.0) * 1.5
GREEN_GAIN = 3.0 / math.sqrt(5.0)
GAMMA = (25.0 / 36.0) * GREEN_GAIN * (1.0 - ROOT * ROOT)
EPS = (1.0 / 12.0) / GAMMA
VISCOSITY = 0.2
RELAX_TIME = 1.0
TIME_STEP = 0.5
LOADING = 0.5
WINDOW = 96
F32 = jnp.float32
BF16 = jnp.bfloat16
VMEM_LIMIT = 54 * 1024 * 1024


def iota(shape, dim):
    return lax.broadcasted_iota(jnp.int32, shape, dim)


def dot(a, b, ca, cb):
    return lax.dot_general(a, b, (((ca,), (cb,)), ((), ())), preferred_element_type=F32)


def end_lanes(span):
    corner = (8, span)
    first = (iota(corner, 0) == 0) & (iota(corner, 1) == 0)
    second = (iota(corner, 0) == 1) & (iota(corner, 1) == span - 1)
    return jnp.where(first | second, 1.0, 0.0)


def request_slots(kt, capacity, devices, owner_row, index_row):
    count = owner_row.shape[1]
    blocks = count // kt
    rows, cols = iota((count, count), 0), iota((count, count), 1)
    pick = cols == kt * (rows % blocks) + rows // blocks
    owner = jnp.sum(jnp.where(pick, owner_row, 0), 1, keepdims=True)
    index = jnp.sum(jnp.where(pick, index_row, 0), 1, keepdims=True)
    onehot = (owner == iota((count, devices), 1)).astype(F32)
    lower = (cols <= rows).astype(F32).astype(BF16)
    seen = dot(lower, onehot.astype(BF16), 1, 0)
    position = jnp.sum(seen * onehot, 1, keepdims=True).astype(jnp.int32) - 1
    place = position == iota((count, 128), 1)
    high = jnp.where(place, (index // 128).astype(F32), 0.0).astype(BF16)
    low = jnp.where(place, (index % 128).astype(F32), 0.0).astype(BF16)
    turned = onehot.astype(BF16)
    high_sum, low_sum = dot(turned, high, 0, 0), dot(turned, low, 0, 0)
    send = high_sum.astype(jnp.int32) * 128 + low_sum.astype(jnp.int32)
    return owner * capacity + position, send


def row_fields(ref, i):
    u = [ref[c, i] for c in range(3)]
    return u + [u[0] * u[c] for c in range(3)]


def exchange_kernel(
    sizes, owner_ref, index_ref, field_hbm,
    reply_ref, slot_ref, got_ref, right_ref, part_hbm,
    field_ref, table_ref, send_ref, got_smem, rows_ref, tile_ref, my_low, my_high, my_left, my_right,
    low_ref, high_ref, left_ref, halo_ref, part_ref,
    field_sem, smem_sem, send_sem, recv_sem, tile_send, tile_recv, edge_send, edge_recv, part_sem,
):
    gx, gz, kt, capacity, window = sizes
    devices = gx * gz
    wall, span = my_left.shape[1:]
    lines = field_ref.shape[1]
    slab = lines // wall
    x, z = lax.axis_index("gx"), lax.axis_index("gz")
    me = x * gz + z
    fetch = pltpu.make_async_copy(field_hbm, field_ref, field_sem)
    fetch.start()

    barrier = pltpu.get_barrier_semaphore()

    def greet(d, carry):
        peer = lax.rem(me + d, devices)
        pl.semaphore_signal(
            barrier, inc=1, device_id=(peer // gz, lax.rem(peer, gz)), device_id_type=pl.DeviceIdType.MESH
        )
        return carry

    lax.fori_loop(1, devices, greet, 0)
    slot, send = request_slots(kt, capacity, devices, owner_ref[...], index_ref[...])
    slot_ref[...] = slot
    table_ref[...] = send
    for d in range(devices):
        send_ref[d] = table_ref[d : d + 1, :]
    pl.semaphore_wait(barrier, devices - 1)

    def parcel(d):
        peer = lax.rem(me + d, devices)
        return pltpu.make_async_remote_copy(
            src_ref=send_ref.at[peer],
            dst_ref=got_ref.at[me],
            send_sem=send_sem.at[d],
            recv_sem=recv_sem.at[d],
            device_id=(peer // gz, lax.rem(peer, gz)),
            device_id_type=pl.DeviceIdType.MESH,
        )

    def post(d, carry):
        parcel(d).start()
        return carry

    lax.fori_loop(1, devices, post, 0)
    got_ref[me] = send_ref[me]
    fetch.wait()

    def arrive(d, carry):
        parcel(d).wait()
        return carry

    lax.fori_loop(1, devices, arrive, 0)
    copy = pltpu.make_async_copy(got_ref, got_smem, smem_sem)
    copy.start()
    copy.wait()

    def collect(peer):
        for k in range(capacity):
            row = jnp.minimum(jnp.maximum(got_smem[peer, 0, k], 0), lines - 1)
            for c in range(3):
                rows_ref[c, k : k + 1, :] = field_ref[c, pl.ds(row, 1), :]
        return [rows_ref[c].astype(BF16) for c in range(3)]

    def tiles(d):
        peer = lax.rem(me + d, devices)
        return pltpu.make_async_remote_copy(
            src_ref=tile_ref.at[peer],
            dst_ref=reply_ref.at[me],
            send_sem=tile_send.at[d],
            recv_sem=tile_recv.at[d],
            device_id=(peer // gz, lax.rem(peer, gz)),
            device_id_type=pl.DeviceIdType.MESH,
        )

    def gather(d, carry):
        peer = lax.rem(me + d, devices)
        for c, value in enumerate(collect(peer)):
            tile_ref[peer, :, c * span : (c + 1) * span] = value
        tiles(d).start()
        return carry

    lax.fori_loop(1, devices, gather, 0)
    for c, value in enumerate(collect(me)):
        reply_ref[me, :, c * span : (c + 1) * span] = value

    def edge(k, src, dst, peer):
        return pltpu.make_async_remote_copy(
            src_ref=src,
            dst_ref=dst,
            send_sem=edge_send.at[k],
            recv_sem=edge_recv.at[k],
            device_id=peer,
            device_id_type=pl.DeviceIdType.MESH,
        )

    edges = [
        edge(0, my_right, left_ref, (lax.rem(x + 1, gx), z)),
        edge(1, my_left, right_ref, (lax.rem(x + gx - 1, gx), z)),
        edge(2, my_high, low_ref, (x, lax.rem(z + 1, gz))),
        edge(3, my_low, high_ref, (x, lax.rem(z + gz - 1, gz))),
    ]

    def load(i):
        at = pl.ds(pl.multiple_of(i * wall, wall), wall)
        u = [field_ref[c, at, :] for c in range(3)]
        return u + [u[0] * u[c] for c in range(3)]

    def moments(order):
        def one(i, state):
            return tuple(f + ROOT * s for f, s in zip(load(order(i)), state))

        return lax.fori_loop(0, window, one, (jnp.zeros((wall, span), F32),) * 6, unroll=4)

    for k, value in enumerate(moments(lambda i: slab - window + i)):
        my_right[k] = value
    for c in range(3):
        my_right[6 + c] = field_ref[c, lines - wall :, :]
    edges[0].start()
    pick = end_lanes(span).astype(BF16)
    for c in range(3):
        for n in range(slab // window):
            part = slice(n * window * wall, (n + 1) * window * wall)
            lanes = dot(pick, field_ref[c, part].astype(BF16), 1, 1)
            my_low[c, :, part] = lanes[0:1]
            my_high[c, :, part] = lanes[1:2]
    edges[2].start()
    edges[3].start()
    for k, value in enumerate(moments(lambda i: window - 1 - i)):
        my_left[k] = value
    for c in range(3):
        my_left[6 + c] = field_ref[c, :wall, :]
    edges[1].start()
    for k in (0, 2, 3):
        edges[k].wait()

    rows = halo_ref.shape[1] // wall
    lane = iota((wall, span), 1)
    shape = (8, rows * wall)
    first, second = iota(shape, 0) == 0, iota(shape, 0) == 1

    def leave(n):
        at = pl.ds(pl.multiple_of(n * rows * wall, rows * wall), rows * wall)
        return pltpu.make_async_copy(part_ref.at[:, at, :], part_hbm.at[:, at, :], part_sem.at[n])

    def chunk(n, carry):
        at = pl.ds(pl.multiple_of(n * rows * wall, rows * wall), rows * wall)
        for c in range(3):
            ends = jnp.where(first, low_ref[c, :, at], jnp.where(second, high_ref[c, :, at], 0.0))
            halo_ref[c] = dot(ends.astype(BF16), pick, 0, 0)

        def one(i, carry):
            fields, sums, carry = advance(load(n * rows + i), carry)
            here = pl.ds(pl.multiple_of((n * rows + i) * wall, wall), wall)
            for c in range(3):
                u = fields[c]
                near = jnp.where(lane == 0, 0.0, pltpu.roll(u, 1, 1))
                far = jnp.where(lane == span - 1, 0.0, pltpu.roll(u, span - 1, 1))
                edge_part = halo_ref[c, pl.ds(pl.multiple_of(i * wall, wall), wall), :]
                curve = near + far + edge_part - 2.0 * u
                part_ref[c, here, :] = 0.5 * GAMMA * sums[c] + VISCOSITY * curve
            return carry

        carry = lax.fori_loop(0, rows, one, carry, unroll=4)
        leave(n).start()
        return carry

    border = [left_ref[6 + c] for c in range(3)]
    border = border + [border[0] * border[c] for c in range(3)]
    lax.fori_loop(0, slab // rows, chunk, tuple(left_ref[k] for k in range(6)) + tuple(border))

    def finish(n, carry):
        leave(n).wait()
        return carry

    lax.fori_loop(0, slab // rows, finish, 0)
    edges[1].wait()

    def receive(d, carry):
        tiles(d).wait()
        return carry

    lax.fori_loop(1, devices, receive, 0)


def load_state(state_ref, edge_ref):
    edge = [edge_ref[6 + c] for c in range(3)]
    edge = edge + [edge[0] * edge[c] for c in range(3)]
    for k in range(6):
        state_ref[k] = edge_ref[k]
        state_ref[6 + k] = edge[k]


def advance(fields, carry):
    state, before = carry[:6], carry[6:]
    parts = [EPS * f + s for f, s in zip(before, state)]
    sums = [parts[3 + c] + fields[0] * parts[c] for c in range(3)]
    moved = [f + ROOT * s for f, s in zip(fields, state)]
    return fields, sums, tuple(moved) + tuple(fields)


def down_kernel(u_ref, part_ref, right_ref, out_ref, state_ref):
    rows = u_ref.shape[1]

    @pl.when(pl.program_id(0) == 0)
    def _():
        load_state(state_ref, right_ref)

    def one(n, carry):
        i = rows - 1 - n
        _, sums, carry = advance(row_fields(u_ref, i), carry)
        for c in range(3):
            out_ref[c, i] = part_ref[c, i] - 0.5 * GAMMA * sums[c]
        return carry

    end = lax.fori_loop(0, rows, one, tuple(state_ref[k] for k in range(12)), unroll=4)
    for k in range(12):
        state_ref[k] = end[k]


def particle_kernel(kt, live_ref, slot_ref, reply_ref, weight_ref, velocity_ref, moved_ref, out_ref, own_ref, push_ref):
    step, last = pl.program_id(0), pl.num_programs(0) - 1
    group, particles, cells = weight_ref.shape
    count, slots = slot_ref.shape[0], reply_ref.shape[0]
    span = cells // kt
    blocks = count // kt

    @pl.when(step == 0)
    def _():
        chosen = jnp.where(slot_ref[...] == iota((count, slots), 1), 1.0, 0.0).astype(BF16)
        own = dot(chosen, reply_ref[...], 1, 0)
        for j in range(kt):
            for c in range(3):
                own_ref[c, :, j * span : (j + 1) * span] = own[
                    j * blocks : (j + 1) * blocks, c * span : (c + 1) * span
                ]

    base = pl.multiple_of(step * group, group)
    tiles = jnp.concatenate([own_ref[c, pl.ds(base, group), :] for c in range(3)], 0).astype(BF16)
    row = iota((3 * group, particles), 0) % group
    sampled = jnp.zeros((3 * group, particles), F32)
    for b in range(0, group, 2):
        both = dot(tiles, weight_ref[b : b + 2].reshape(2 * particles, cells), 1, 1)
        sampled = jnp.where(row == b, both[:, :particles], sampled)
        sampled = jnp.where(row == b + 1, both[:, particles:], sampled)
    velocity = velocity_ref[...].reshape(3 * group, particles)
    live = jnp.where(row + base < live_ref[0], 1.0, 0.0)
    drag = live * (sampled - velocity) * (1.0 / RELAX_TIME)
    moved_ref[...] = (velocity + TIME_STEP * drag).reshape(3, group, particles)
    half = drag.astype(BF16)
    row = iota((3 * group, cells), 0) % group
    push = jnp.zeros((3 * group, cells), F32)
    for b in range(group):
        push = jnp.where(row == b, dot(half, weight_ref[b], 1, 0), push)
    push = -LOADING * push
    for j in range(kt):
        for c in range(3):
            push_ref[pl.ds(j * blocks + base, group), c * span : (c + 1) * span] = push[
                c * group : (c + 1) * group, j * span : (j + 1) * span
            ]

    @pl.when(step == last)
    def _():
        same = iota((count, count), 0) == iota((count, count), 1)
        slot_row = jnp.sum(jnp.where(same, slot_ref[...], 0), 0, keepdims=True)
        placed = jnp.where(iota((slots, count), 0) == slot_row, 1.0, 0.0).astype(BF16)
        out_ref[...] = dot(placed, push_ref[...].astype(BF16), 1, 0).astype(BF16)


def add_kernel(index_ref, base_ref, back_ref, out_ref):
    rows, span = base_ref.shape[1:]
    slots = back_ref.shape[0]
    for n in range(rows // 256):
        local = index_ref[...] - (pl.program_id(0) * rows + n * 256)
        local = jnp.where((local >= 0) & (local < 256), local, -1).astype(F32).astype(BF16)
        ids = iota((256, slots), 0).astype(F32).astype(BF16)
        named = jnp.where(ids == local, jnp.ones((), BF16), jnp.zeros((), BF16))
        total = dot(named, back_ref[...], 1, 0)
        part = slice(n * 256, (n + 1) * 256)
        for c in range(3):
            out_ref[c, part] = base_ref[c, part] + total[:, c * span : (c + 1) * span]


def vmem():
    return pl.BlockSpec(memory_space=pltpu.VMEM)


def smem():
    return pl.BlockSpec(memory_space=pltpu.SMEM)


def params(mebibytes):
    return pltpu.CompilerParams(vmem_limit_bytes=mebibytes * 1024 * 1024)


def cost(flops, nbytes):
    return pl.CostEstimate(flops=int(flops), bytes_accessed=int(nbytes), transcendentals=0)


def largest_divisor(total, limit):
    return max(d for d in range(1, limit + 1) if total % d == 0)


def shards(velocity_field, interp_weight, particle_velocity, tile_owner, tile_index, block_count):
    _, slab, wall, span = velocity_field.shape
    shape = jax.ShapeDtypeStruct
    gx, gz = lax.axis_size("gx"), lax.axis_size("gz")
    devices = gx * gz
    requests = tile_index.shape[0]
    blocks, particles, cells = interp_weight.shape
    kt = requests // blocks
    capacity = max(2, 3 * requests // devices)
    slots = devices * capacity
    field_bytes = velocity_field.size * 4

    window = WINDOW if slab % WINDOW == 0 else slab
    lines = slab * wall
    dma = pltpu.SemaphoreType.DMA
    rows = largest_divisor(slab, 48)
    parts = slab // rows
    replies, slot_ids, got, from_right, up_part = pl.pallas_call(
        functools.partial(exchange_kernel, (gx, gz, kt, capacity, window)),
        out_shape=(
            shape((devices, capacity, 3 * span), BF16),
            shape((requests, 1), jnp.int32),
            shape((devices, 1, 128), jnp.int32),
            shape((9, wall, span), F32),
            shape((3, lines, span), F32),
        ),
        in_specs=[vmem(), vmem(), pl.BlockSpec(memory_space=pl.ANY)],
        out_specs=(vmem(),) * 4 + (pl.BlockSpec(memory_space=pl.ANY),),
        scratch_shapes=[
            pltpu.VMEM((3, lines, span), F32),
            pltpu.VMEM((devices, 128), jnp.int32),
            pltpu.VMEM((devices, 1, 128), jnp.int32),
            pltpu.SMEM((devices, 1, 128), jnp.int32),
            pltpu.VMEM((3, capacity, span), F32),
            pltpu.VMEM((devices, capacity, 3 * span), BF16),
            pltpu.VMEM((3, 1, lines), F32),
            pltpu.VMEM((3, 1, lines), F32),
            pltpu.VMEM((9, wall, span), F32),
            pltpu.VMEM((9, wall, span), F32),
            pltpu.VMEM((3, 1, lines), F32),
            pltpu.VMEM((3, 1, lines), F32),
            pltpu.VMEM((9, wall, span), F32),
            pltpu.VMEM((3, rows * wall, span), F32),
            pltpu.VMEM((3, lines, span), F32),
            dma,
            dma,
            dma((devices,)),
            dma((devices,)),
            dma((devices,)),
            dma((devices,)),
            dma((4,)),
            dma((4,)),
            dma((parts,)),
        ],
        compiler_params=pltpu.CompilerParams(
            vmem_limit_bytes=VMEM_LIMIT, collective_id=0, has_side_effects=True
        ),
        cost_estimate=cost(1e7, field_bytes),
        name="exchange",
    )(tile_owner.reshape(1, requests), tile_index.reshape(1, requests), velocity_field.reshape(3, lines, span))
    got = got[:, 0, :capacity].reshape(1, slots)
    replies = replies.reshape(slots, 3 * span)
    up_part = up_part.reshape(velocity_field.shape)

    group = 16 if blocks % 16 == 0 else 8
    moved, outgoing = pl.pallas_call(
        functools.partial(particle_kernel, kt),
        grid=(blocks // group,),
        out_shape=(shape(particle_velocity.shape, F32), shape((slots, 3 * span), BF16)),
        in_specs=[
            smem(),
            pl.BlockSpec((requests, 1), lambda i: (0, 0)),
            pl.BlockSpec((slots, 3 * span), lambda i: (0, 0)),
            pl.BlockSpec((group, particles, cells), lambda i: (i, 0, 0)),
            pl.BlockSpec((3, group, particles), lambda i: (0, i, 0)),
        ],
        out_specs=(
            pl.BlockSpec((3, group, particles), lambda i: (0, i, 0)),
            pl.BlockSpec((slots, 3 * span), lambda i: (0, 0)),
        ),
        scratch_shapes=[
            pltpu.VMEM((3, blocks, cells), F32),
            pltpu.VMEM((requests, 3 * span), F32),
        ],
        compiler_params=params(16),
        cost_estimate=cost(4e8, interp_weight.size * 2),
        name="particles",
    )(block_count, slot_ids, replies, interp_weight, particle_velocity)
    outgoing, up_part = lax.optimization_barrier((outgoing, up_part))
    returned = lax.all_to_all(outgoing, ("gx", "gz"), split_axis=0, concat_axis=0, tiled=True)
    fluid = pl.pallas_call(
        down_kernel,
        grid=(parts,),
        out_shape=shape(velocity_field.shape, F32),
        in_specs=[
            pl.BlockSpec((3, rows, wall, span), lambda i: (0, parts - 1 - i, 0, 0)),
            pl.BlockSpec((3, rows, wall, span), lambda i: (0, parts - 1 - i, 0, 0)),
            pl.BlockSpec((9, wall, span), lambda i: (0, 0, 0)),
        ],
        out_specs=pl.BlockSpec((3, rows, wall, span), lambda i: (0, parts - 1 - i, 0, 0)),
        scratch_shapes=[pltpu.VMEM((12, wall, span), F32)],
        compiler_params=params(56),
        cost_estimate=cost(velocity_field.size * 20, field_bytes * 3),
        name="down",
    )(velocity_field, up_part, from_right)

    chunk = 1024 if lines % 1024 == 0 else lines
    result = pl.pallas_call(
        add_kernel,
        grid=(lines // chunk,),
        out_shape=shape((3, lines, span), F32),
        in_specs=[
            pl.BlockSpec((1, slots), lambda i: (0, 0)),
            pl.BlockSpec((3, chunk, span), lambda i: (0, i, 0)),
            pl.BlockSpec((slots, 3 * span), lambda i: (0, 0)),
        ],
        out_specs=pl.BlockSpec((3, chunk, span), lambda i: (0, i, 0)),
        compiler_params=params(56),
        cost_estimate=cost(2.0 * lines * slots * 3 * span, field_bytes * 2),
        name="feedback",
    )(got, fluid.reshape(3, lines, span), returned)
    return (result.reshape(velocity_field.shape), moved)


def solution(mesh):
    placed = (
        P(None, "gx", None, "gz"),
        P(("gx", "gz"), None, None),
        P(None, ("gx", "gz"), None),
        P(("gx", "gz"), None),
        P(("gx", "gz")),
        P(("gx", "gz")),
    )
    return jax.shard_map(
        shards,
        mesh=mesh,
        in_specs=placed,
        out_specs=(P(None, "gx", None, "gz"), P(None, ("gx", "gz"), None)),
        check_vma=False,
    )
```
